1024 devices in a mesh: row: 32 (over z), col: 32 (over x, y, core).
Axes of the slice: x: 4, y: 4, z: 32, core: 2. Of those that a mesh axis runs over, the one named last changes fastest.
Arguments:
- momentum: float32 [16384, 16384], P('row', 'col'), may hold values from -18 to 18
- gradient: bfloat16 [16384, 16384], P('row', 'col'), may hold values from -6 to 6
- right_factor: float32 [16384, 64], P('col'), may hold values from -1 to 1
Outputs:
- update: bfloat16 [16384, 16384], P('row', 'col')
- left: float32 [16384, 64], P('row')
- normed: float32 [16384, 64], P('col')
- new_momentum: float32 [16384, 16384], P('row', 'col')
- first_factor: float32 [64, 64], replicated
The draws below stay inside these ranges and needn't reach their ends.
All inputs are finite; a program needn't handle non-finite values.
Results may differ from the reference program's by a relative error of at most 0.001.
Values sent between devices are 32-bit elements; how exact they have to be, the bound alone decides.
No kernel may reach another device: no remote copies, remote signals or barrier semaphores. Data moves between devices by JAX's collectives and lax.ppermute only.
A program may use at most 32 MiB of HBM per device.

```python
import math
import jax
import jax.numpy as jnp
from jax import lax

NROW = 16384
NCOL = 16384
RANK = 64


def draw_right_factor(key, part):
    key_common = jax.random.fold_in(key, 11)
    key_own = jax.random.fold_in(key, 23)
    key_gain = jax.random.fold_in(key, 37)
    key_spread = jax.random.fold_in(key, 41)
    common = jax.random.truncated_normal(key_common, -5.0, 5.0, (NCOL,), jnp.float32)
    own = jax.random.truncated_normal(key_own, -5.0, 5.0, (NCOL, RANK), jnp.float32)
    gains = jax.random.uniform(key_gain, (RANK,), jnp.float32, 0.7, 1.3)
    spread = jnp.exp(jax.random.uniform(key_spread, (RANK,), jnp.float32, math.log(0.015), math.log(0.05)))
    raw = common[:, None] * gains[None, :] + own * spread[None, :]
    return (raw / jnp.max(jnp.abs(raw))).astype(jnp.float32)


def draw_momentum(key, part):
    key_values = jax.random.fold_in(key, 53)
    position = jnp.arange(NROW, dtype=jnp.float32) / jnp.float32(NROW)
    values = jax.random.truncated_normal(key_values, -6.0, 6.0, (NROW, NCOL), jnp.float32)
    row_scale = jnp.exp(position * math.log(3.0))
    return (values * row_scale[:, None]).astype(jnp.float32)


def level_of(rng, shape, cuts, low, largest):
    def one(axis_at, shards_of):
        heights = jax.random.uniform(jax.random.fold_in(jax.random.fold_in(rng, 6), axis_at), (shards_of,), jnp.float32, low / len(cuts), largest / len(cuts))
        return jnp.repeat(jnp.exp(heights), shape[axis_at] // shards_of).reshape((-1,) + (1,) * (len(shape) - axis_at - 1))

    gain = one(*cuts[0])
    for cut in cuts[1:]:
        gain = gain * one(*cut)
    return gain


def gaussian(own_key, shape, width, reach, shards=(), held_as=jnp.bfloat16):
    values = jax.random.normal(own_key, shape, jnp.float32) * width
    if len(shards) > 0:
        values = level_of(own_key, shape, shards, -0.22, 0.18) * values
    return jnp.clip(values, min=-reach, max=reach).astype(held_as)


def setup_inputs(seed: int = 0) -> dict:
    key_of = jax.random.split(jax.random.key(seed), 4)
    return {
        "momentum": draw_momentum(jax.random.fold_in(key_of[3], 71), 0),
        "gradient": gaussian(key_of[1], (NROW, NCOL), 1.0, 6.0, ((0, 32), (1, 32))),
        "right_factor": draw_right_factor(jax.random.fold_in(key_of[3], 71), 0),
    }


HIGH = lax.Precision.HIGHEST

def cholesky_parts(raw):
    gram = jnp.dot(raw.T.astype(jnp.float32), raw.astype(jnp.float32), precision=HIGH, preferred_element_type=jnp.float32)
    lower = jnp.linalg.cholesky(gram)
    solved = lax.linalg.triangular_solve(lower, raw, left_side=False, lower=True, transpose_a=True)
    return (solved, lower)

def reference(momentum, gradient, right_factor):
    blended = momentum + gradient.astype(jnp.float32)
    left_raw = jnp.dot(blended.astype(jnp.float32), right_factor.astype(jnp.float32), precision=HIGH, preferred_element_type=jnp.float32)
    left_one, lower_one = cholesky_parts(left_raw)
    first_factor = lower_one / jnp.sqrt(jnp.float32(NROW) * jnp.float32(NCOL))
    left, lower_two = cholesky_parts(left_one)
    right = lax.dot_general(blended.astype(jnp.float32), left.astype(jnp.float32), (((0,), (0,)), ((), ())), precision=HIGH, preferred_element_type=jnp.float32)
    norms = jnp.sqrt(lax.optimization_barrier(jnp.sum(right * right, axis=0)))
    normed = right / (norms + 1e-06)
    scale = jnp.sqrt(jnp.float32(NROW) * jnp.float32(NCOL) / jnp.float32(RANK))
    update = (scale * jnp.dot(left.astype(jnp.float32), normed.T.astype(jnp.float32), precision=HIGH, preferred_element_type=jnp.float32)).astype(jnp.bfloat16)
    new_momentum = blended - 0.05 * jnp.dot(left.astype(jnp.float32), right.T.astype(jnp.float32), precision=HIGH, preferred_element_type=jnp.float32)
    return (update, left, normed, new_momentum, first_factor)
```

```python
import jax
import jax.numpy as jnp
from jax import lax
from jax.sharding import Mesh, PartitionSpec as P

NROW = 16384
NCOL = 16384
RANK = 64
HIGH = lax.Precision.HIGHEST
COL = ("x", "y", "core")
NEAR = ("near",)
FAR = ("far",)


def dot(a, b, dims):
    return lax.dot_general(
        a, b, (dims, ((), ())), precision=HIGH, preferred_element_type=jnp.float32
    )


def nn(a, b):
    return dot(a, b, ((1,), (0,)))


def nt(a, b):
    return dot(a, b, ((1,), (1,)))


def to_tiles(a):
    return a.reshape(8, 8, 4, 128).transpose(0, 2, 1, 3).reshape(32, 8, 128)


def from_tiles(t):
    return t.reshape(8, 4, 8, 128).transpose(0, 2, 1, 3).reshape(64, 512)


def exchange(chunks, axes):
    return lax.all_to_all(chunks, axes, 0, 0, tiled=True)


def spread(chunk, n, axes):
    copies = jnp.broadcast_to(chunk[None], (n,) + chunk.shape)
    return exchange(lax.optimization_barrier(copies), axes)


def lower_and_inverse(gram):
    lower = jnp.linalg.cholesky(gram)
    inverse = lax.linalg.triangular_solve(
        lower, jnp.eye(RANK, dtype=jnp.float32), left_side=True, lower=True
    )
    return lower, inverse


def on_device(momentum, gradient, right_factor):
    blended = momentum + gradient.astype(jnp.float32)
    factor_t = right_factor.T
    part = to_tiles(nt(factor_t, blended))
    mine = jnp.sum(exchange(part, COL), axis=0)
    left_raw_t = from_tiles(spread(mine, 32, COL))
    product = to_tiles(nn(left_raw_t, blended)).reshape(256, 128)
    gram = nt(left_raw_t, left_raw_t)
    gram = jnp.concatenate([gram[:32], gram[32:]], axis=1)
    send = jnp.concatenate([product, gram], axis=0).reshape(4, 72, 128)
    near = jnp.sum(exchange(send, NEAR), axis=0)
    total = spread(lax.psum(near, FAR), 4, NEAR).reshape(288, 128)
    product_t = from_tiles(total[:256].reshape(32, 8, 128))
    gram_one = jnp.concatenate([total[256:, :64], total[256:, 64:]], axis=0)
    gram_one = (gram_one + gram_one.T) / 2
    lower_one, inverse_one = lower_and_inverse(gram_one)
    first_factor = lower_one / jnp.sqrt(jnp.float32(NROW) * jnp.float32(NCOL))
    factor_one = nn(inverse_one, factor_t)
    right_one = nn(inverse_one, product_t)
    pair = jnp.concatenate([nt(factor_one, right_one), nt(right_one, right_one)], axis=1)
    pair = jnp.sum(spread(pair, 32, COL), axis=0)
    gram_two, squared = pair[:, :64], pair[:, 64:]
    gram_two = (gram_two + gram_two.T) / 2
    _, inverse_two = lower_and_inverse(gram_two)
    left_one = nn(inverse_one, left_raw_t)
    left_t = nn(inverse_two, left_one)
    right_t = nn(inverse_two, right_one)
    squares = jnp.sum(nn(inverse_two, squared) * inverse_two, axis=1)
    normed_t = right_t / (jnp.sqrt(squares) + 1e-06)[:, None]
    scale = jnp.sqrt(jnp.float32(NROW) * jnp.float32(NCOL) / jnp.float32(RANK))
    tn = lambda a, b: dot(a, b, ((0,), (0,)))
    update = (scale * tn(left_t, normed_t)).astype(jnp.bfloat16)
    new_momentum = blended - 0.05 * tn(left_t, right_t)
    return (update, left_t.T, normed_t.T, new_momentum, first_factor)


def solution(mesh):
    names = FAR + NEAR + COL
    inner = Mesh(mesh.devices.reshape(8, 4, 4, 4, 2), names)
    row, col = FAR + NEAR, COL
    in_specs = (P(row, col), P(row, col), P(col, None))
    out_specs = (P(row, col), P(row, None), P(col, None), P(row, col), P())
    return jax.shard_map(
        on_device, mesh=inner, in_specs=in_specs, out_specs=out_specs, check_vma=False
    )
```

```python
import functools
import math

import jax
import jax.numpy as jnp
from jax import lax
from jax.experimental import pallas as pl
from jax.experimental.pallas import tpu as pltpu
from jax.sharding import Mesh, PartitionSpec as P

NROW = 16384
NCOL = 16384
RANK = 64
HIGH = lax.Precision.HIGHEST
COL = ("x", "y", "core")
NEAR = ("near",)
FAR = ("far",)
SIDE = 512
F32 = jnp.float32


def dot(a, b, dims):
    return lax.dot_general(
        a, b, (dims, ((), ())), precision=HIGH, preferred_element_type=F32
    )


def nn(a, b):
    return dot(a, b, ((1,), (0,)))


def nt(a, b):
    return dot(a, b, ((1,), (1,)))


def tn(a, b):
    return dot(a, b, ((0,), (0,)))


def call(kernel, outs, *args):
    whole = pl.BlockSpec(memory_space=pltpu.VMEM)
    return pl.pallas_call(
        kernel,
        out_shape=[jax.ShapeDtypeStruct(s, d) for s, d in outs],
        in_specs=[whole] * len(args),
        out_specs=[whole] * len(outs),
        name=kernel.__name__,
    )(*args)


def write_tiles(ref, a):
    for i in range(8):
        for j in range(4):
            ref[4 * i + j] = a[8 * i : 8 * i + 8, 128 * j : 128 * j + 128]


def read_tiles(ref):
    rows = [jnp.concatenate([ref[4 * i + j] for j in range(4)], axis=1) for i in range(8)]
    return jnp.concatenate(rows, axis=0)


def places(shape):
    return lax.broadcasted_iota(jnp.int32, shape, 0), lax.broadcasted_iota(jnp.int32, shape, 1)


def fold(a):
    return jnp.concatenate([a[:32], a[32:]], axis=1)


def unfold(a):
    return jnp.concatenate([a[:, :64], a[:, 64:]], axis=0)


def factor(gram):
    row, lane = places((RANK, RANK))
    eye = jnp.where(row == lane, 1.0, 0.0).astype(F32)
    both = jnp.concatenate([gram, eye], axis=1)
    blocks = [both[8 * b : 8 * b + 8] for b in range(8)]
    in_block, _ = places((8, 128))
    for k in range(RANK - 1):
        at, r = divmod(k, 8)
        line = blocks[at][r : r + 1]
        line = line / line[:, k : k + 1]
        for b in range(at, 8):
            column = blocks[b][:, k : k + 1]
            if b == at:
                if r == 7:
                    continue
                column = jnp.where(in_block > r, column, 0.0)
            blocks[b] = blocks[b] - column * line
    both = jnp.concatenate(blocks, axis=0)
    upper, inverse = both[:, :64], both[:, 64:]
    pivot = jnp.sum(jnp.where(row == lane, upper, 0.0), axis=1, keepdims=True)
    root = 1.0 / jnp.sqrt(pivot)
    upper = jnp.where(row <= lane, upper * root, 0.0)
    return upper, inverse * root


def left_part(momentum, gradient, factor_t, part):
    blended = momentum[...] + gradient[...].astype(F32)
    write_tiles(part, nt(factor_t[...], blended))


def left_tile(parts, copies):
    tile = jnp.sum(parts[...], axis=0)
    for i in range(32):
        copies[i] = tile


def right_part(tiles, momentum, gradient, send):
    left_raw = read_tiles(tiles)
    blended = momentum[...] + gradient[...].astype(F32)
    write_tiles(send, nn(left_raw, blended))
    gram = fold(nt(left_raw, left_raw))
    for i in range(4):
        send[32 + i] = gram[8 * i : 8 * i + 8]


def first_pass(total, factor_t, upper_one, inverse_one, right_one, copies):
    gram = unfold(jnp.concatenate([total[32 + i] for i in range(4)], axis=0))
    upper, inverse = factor(gram)
    upper_one[...] = upper
    inverse_one[...] = inverse
    right = nn(inverse, read_tiles(total))
    right_one[...] = right
    gram_two = nt(nn(inverse, factor_t[...]), right)
    squared = nt(right, right)
    row, lane = places((RANK, RANK))
    diagonal = jnp.sum(jnp.where(row == lane, squared, 0.0), axis=0, keepdims=True)
    pair = fold(jnp.where(row <= lane, gram_two, squared))
    last = jnp.concatenate([diagonal, jnp.zeros((1, 64), F32)], axis=1)
    last = jnp.broadcast_to(last, (8, 128))
    for i in range(32):
        copies[i, :32] = pair
        copies[i, 32:] = last


def second_pass(
    pairs, tiles, inverse_one, right_one, momentum, gradient,
    update, left, normed, new_momentum,
):
    pair = jnp.sum(pairs[...], axis=0)
    mixed = unfold(pair[:32])
    diagonal = pair[32:33, :64]
    row, lane = places((RANK, RANK))
    flipped = mixed.T
    gram_two = jnp.where(row <= lane, mixed, flipped)
    squared = jnp.where(row > lane, mixed, flipped)
    squared = jnp.where(row == lane, diagonal, squared)
    _, inverse = factor(gram_two)
    left_t = nn(inverse, nn(inverse_one[...], read_tiles(tiles)))
    right_t = nn(inverse, right_one[...])
    squares = jnp.sum(nn(inverse, squared) * inverse, axis=1, keepdims=True)
    normed_t = right_t / (jnp.sqrt(squares) + 1e-06)
    left[...] = left_t
    normed[...] = normed_t
    scale = math.sqrt(NROW * NCOL / RANK)
    update[...] = (scale * tn(left_t, normed_t)).astype(jnp.bfloat16)
    blended = momentum[...] + gradient[...].astype(F32)
    new_momentum[...] = blended - 0.05 * tn(left_t, right_t)


def exchange(chunks, axes):
    return lax.all_to_all(chunks, axes, 0, 0, tiled=True)


def on_device(momentum, gradient, right_factor):
    factor_t = right_factor.T
    flat = (RANK, SIDE)
    square = (RANK, RANK)
    (part,) = call(left_part, [((32, 8, 128), F32)], momentum, gradient, factor_t)
    (copies,) = call(left_tile, [((32, 8, 128), F32)], exchange(part, COL))
    tiles = exchange(copies, COL)
    (send,) = call(right_part, [((36, 8, 128), F32)], tiles, momentum, gradient)
    near = jnp.sum(exchange(send.reshape(4, 72, 128), NEAR), axis=0)
    far = lax.psum(near, FAR)
    total = exchange(jnp.broadcast_to(far[None], (4, 72, 128)), NEAR).reshape(36, 8, 128)
    upper_one, inverse_one, right_one, copies = call(
        first_pass,
        [(square, F32), (square, F32), (flat, F32), ((32, 40, 128), F32)],
        total,
        factor_t,
    )
    first_factor = upper_one.T / jnp.sqrt(F32(NROW) * F32(NCOL))
    pairs = exchange(copies, COL)
    full = (SIDE, SIDE)
    update, left_t, normed_t, new_momentum = call(
        second_pass,
        [(full, jnp.bfloat16), (flat, F32), (flat, F32), (full, F32)],
        pairs, tiles, inverse_one, right_one, momentum, gradient,
    )
    return (update, left_t.T, normed_t.T, new_momentum, first_factor)


def solution(mesh):
    inner = Mesh(mesh.devices.reshape(8, 4, 4, 4, 2), FAR + NEAR + COL)
    row, col = FAR + NEAR, COL
    in_specs = (P(row, col), P(row, col), P(col, None))
    out_specs = (P(row, col), P(row, None), P(col, None), P(row, col), P())
    return jax.shard_map(
        on_device, mesh=inner, in_specs=in_specs, out_specs=out_specs, check_vma=False
    )
```

```python
import math

import jax
import jax.numpy as jnp
from jax import lax
from jax.experimental import pallas as pl
from jax.experimental.pallas import tpu as pltpu
from jax.sharding import Mesh, PartitionSpec as P

NROW = 16384
NCOL = 16384
RANK = 64
HIGH = lax.Precision.HIGHEST
COL = ("x", "y", "core")
NEAR = ("near",)
FAR = ("far",)
SIDE = 512
F32 = jnp.float32


def dot(a, b, dims):
    return lax.dot_general(
        a, b, (dims, ((), ())), precision=HIGH, preferred_element_type=F32
    )


def nn(a, b):
    return dot(a, b, ((1,), (0,)))


def nt(a, b):
    return dot(a, b, ((1,), (1,)))


def tn(a, b):
    return dot(a, b, ((0,), (0,)))


ANY = pl.BlockSpec(memory_space=pl.ANY)
VMEM = pl.BlockSpec(memory_space=pltpu.VMEM)


def call(kernel, outs, *args, far_in=(), far_out=(), scratch=()):
    args = [
        a if i in far_in else pltpu.with_memory_space_constraint(a, pltpu.VMEM)
        for i, a in enumerate(args)
    ]
    return pl.pallas_call(
        kernel,
        out_shape=[
            jax.ShapeDtypeStruct(s, d) if i in far_out else pltpu.VMEM(s, d)
            for i, (s, d) in enumerate(outs)
        ],
        in_specs=[ANY if i in far_in else VMEM for i in range(len(args))],
        out_specs=[ANY if i in far_out else VMEM for i in range(len(outs))],
        scratch_shapes=list(scratch),
        name=kernel.__name__,
    )(*args)


def write_tiles(ref, a):
    for i in range(8):
        for j in range(4):
            ref[4 * i + j] = a[8 * i : 8 * i + 8, 128 * j : 128 * j + 128]


def read_tiles(ref):
    rows = [jnp.concatenate([ref[4 * i + j] for j in range(4)], axis=1) for i in range(8)]
    return jnp.concatenate(rows, axis=0)


def places(shape):
    return lax.broadcasted_iota(jnp.int32, shape, 0), lax.broadcasted_iota(jnp.int32, shape, 1)


def fold(a):
    return jnp.concatenate([a[:32], a[32:]], axis=1)


def unfold(a):
    return jnp.concatenate([a[:, :64], a[:, 64:]], axis=0)


def factor(gram, width=8):
    row, lane = places((RANK, RANK))
    eye = jnp.where(row == lane, 1.0, 0.0).astype(F32)
    both = jnp.concatenate([gram, eye], axis=1)
    blocks = [both[8 * b : 8 * b + 8] for b in range(8)]
    in_block, _ = places((8, 128))
    for k in range(0, RANK, width):
        at, r = divmod(k, 8)
        columns = [
            {b: jnp.broadcast_to(blocks[b][:, k + j : k + j + 1], (8, 128)) for b in range(at, 8)}
            for j in range(width)
        ]
        lines = [blocks[at][r + j : r + j + 1] for j in range(width)]
        scaled = []
        for j in range(width):
            over = 1.0 / columns[j][at][r + j : r + j + 1]
            scaled.append(lines[j] * over)
            for l in range(j + 1, width):
                share = columns[j][at][r + l : r + l + 1] * over
                lines[l] = lines[l] - share * lines[j]
                for b in range(at, 8):
                    columns[l][b] = columns[l][b] - columns[j][b] * share
        for b in range(at, 8):
            new = blocks[b]
            for j in range(width):
                new = new - columns[j][b] * scaled[j]
            if b == at:
                new = jnp.where(in_block >= r + width, new, blocks[b])
                for j in range(width):
                    new = jnp.where(in_block == r + j, lines[j], new)
            blocks[b] = new
    both = jnp.concatenate(blocks, axis=0)
    upper, inverse = both[:, :64], both[:, 64:]
    pivot = jnp.sum(jnp.where(row == lane, upper, 0.0), axis=1, keepdims=True)
    root = 1.0 / jnp.sqrt(pivot)
    upper = jnp.where(row <= lane, upper * root, 0.0)
    return upper, inverse * root


STEPS = 4
STEP = SIDE // STEPS


def rows_of(i):
    return pl.ds(STEP * i, STEP)


def left_part(momentum, gradient, factor_t, part, blended, old, change, sems):
    copies = [
        pltpu.make_async_copy(momentum, old, sems.at[0]),
        pltpu.make_async_copy(gradient, change, sems.at[1]),
    ]
    for copy in copies:
        copy.start()
    for copy in copies:
        copy.wait()
    block = old[...] + change[...].astype(F32)
    blended[...] = block
    write_tiles(part, nt(factor_t[...], block))


def left_tile(parts, copies):
    tile = jnp.sum(parts[...], axis=0)
    for i in range(32):
        copies[i] = tile


def right_part(tiles, blended, send):
    left_raw = read_tiles(tiles)
    product = nn(left_raw, blended[...])
    gram = fold(nt(left_raw, left_raw))
    for i in range(8):
        for j in range(4):
            tile = product[8 * i : 8 * i + 8, 128 * j : 128 * j + 128]
            send[i // 2, 32 * (i % 2) + 8 * j : 32 * (i % 2) + 8 * j + 8] = tile
    for i in range(4):
        send[i, 64:] = gram


def first_factor_of(gram, upper_one, inverse_one):
    upper, inverse = factor(unfold(gram[...]))
    upper_one[...] = upper
    inverse_one[...] = inverse


def second_gram(total, inverse_one, factor_t, right_one, copies):
    inverse = inverse_one[...]
    right = nn(inverse, read_tiles(total))
    right_one[...] = right
    gram_two = nt(nn(inverse, factor_t[...]), right)
    squared = nt(right, right)
    row, lane = places((RANK, RANK))
    diagonal = jnp.sum(jnp.where(row == lane, squared, 0.0), axis=0, keepdims=True)
    pair = fold(jnp.where(row <= lane, gram_two, squared))
    last = jnp.concatenate([diagonal, jnp.zeros((1, 64), F32)], axis=1)
    last = jnp.broadcast_to(last, (8, 128))
    for i in range(32):
        copies[i, :32] = pair
        copies[i, 32:] = last


def left_once(tiles, inverse_one, left_one):
    left_one[...] = nn(inverse_one[...], read_tiles(tiles))


def halves(a):
    high = a.astype(jnp.bfloat16)
    return high, (a - high.astype(F32)).astype(jnp.bfloat16)


def results(
    pairs, left_one, right_one, blended,
    update, left, normed, new_momentum, u, l, n, m, sems,
):
    pair = jnp.sum(pairs[...], axis=0)
    mixed = unfold(pair[:32])
    diagonal = pair[32:33, :64]
    row, lane = places((RANK, RANK))
    flipped = mixed.T
    gram_two = jnp.where(row <= lane, mixed, flipped)
    squared = jnp.where(row > lane, mixed, flipped)
    squared = jnp.where(row == lane, diagonal, squared)
    _, inverse = factor(gram_two)
    squares = jnp.sum(nn(inverse, squared) * inverse, axis=1, keepdims=True)
    left_t = nn(inverse, left_one[...])
    right_t = nn(inverse, right_one[...])
    normed_t = right_t / (jnp.sqrt(squares) + 1e-06)
    l[...] = left_t
    n[...] = normed_t
    copies = [
        pltpu.make_async_copy(l, left, sems.at[0, 0]),
        pltpu.make_async_copy(n, normed, sems.at[0, 1]),
    ]
    for copy in copies:
        copy.start()
    high, low = halves(left_t)
    lefts = jnp.concatenate([high, high, low], axis=0)
    high, low = halves(0.05 * right_t)
    rights = jnp.concatenate([high, low, high], axis=0)
    high, low = halves(math.sqrt(NROW * NCOL / RANK) * normed_t)
    norms = jnp.concatenate([high, low, high], axis=0)

    def product(i, other):
        part = lefts[:, STEP * i : STEP * i + STEP]
        return lax.dot_general(
            part, other, (((0,), (0,)), ((), ())), preferred_element_type=F32
        )

    for i in range(STEPS):
        m[rows_of(i)] = blended[rows_of(i)] - product(i, rights)
        u[rows_of(i)] = product(i, norms).astype(jnp.bfloat16)
        for k, (source, target) in enumerate(((m, new_momentum), (u, update))):
            copy = pltpu.make_async_copy(
                source.at[rows_of(i)], target.at[rows_of(i)], sems.at[1 + i, k]
            )
            copy.start()
            copies.append(copy)
    for copy in copies:
        copy.wait()


def exchange(chunks, axes):
    return lax.all_to_all(chunks, axes, 0, 0, tiled=True)


def on_device(momentum, gradient, right_factor):
    factor_t = right_factor.T
    flat, square, full = (RANK, SIDE), (RANK, RANK), (SIDE, SIDE)
    tiled = ((32, 8, 128), F32)
    part, blended = call(
        left_part,
        [tiled, (full, F32)],
        momentum, gradient, factor_t,
        far_in=(0, 1),
        scratch=[
            pltpu.VMEM(full, F32),
            pltpu.VMEM(full, jnp.bfloat16),
            pltpu.SemaphoreType.DMA((2,)),
        ],
    )
    (copies,) = call(left_tile, [tiled], exchange(part, COL))
    tiles = exchange(copies, COL)
    (send,) = call(right_part, [((4, 96, 128), F32)], tiles, blended)
    near = jnp.sum(exchange(send, NEAR), axis=0)
    far = lax.psum(near, FAR)
    quarters = jnp.broadcast_to(far[None, :64], (4, 64, 128))
    total = exchange(quarters, NEAR).reshape(32, 8, 128)
    upper_one, inverse_one = call(
        first_factor_of, [(square, F32), (square, F32)], far[64:]
    )
    first_factor = upper_one.T / jnp.sqrt(F32(NROW) * F32(NCOL))
    right_one, copies = call(
        second_gram, [(flat, F32), ((32, 40, 128), F32)], total, inverse_one, factor_t
    )
    pairs = exchange(copies, COL)
    (left_one,) = call(left_once, [(flat, F32)], tiles, inverse_one)
    update, left_t, normed_t, new_momentum = call(
        results,
        [(full, jnp.bfloat16), (flat, F32), (flat, F32), (full, F32)],
        pairs, left_one, right_one, blended,
        far_out=(0, 1, 2, 3),
        scratch=[
            pltpu.VMEM(full, jnp.bfloat16),
            pltpu.VMEM(flat, F32),
            pltpu.VMEM(flat, F32),
            pltpu.VMEM(full, F32),
            pltpu.SemaphoreType.DMA((1 + STEPS, 2)),
        ],
    )
    return (update, left_t.T, normed_t.T, new_momentum, first_factor)


def solution(mesh):
    inner = Mesh(mesh.devices.reshape(8, 4, 4, 4, 2), FAR + NEAR + COL)
    row, col = FAR + NEAR, COL
    in_specs = (P(row, col), P(row, col), P(col, None))
    out_specs = (P(row, col), P(row, None), P(col, None), P(row, col), P())
    return jax.shard_map(
        on_device, mesh=inner, in_specs=in_specs, out_specs=out_specs, check_vma=False
    )
```

```python
import math

import jax
import jax.numpy as jnp
from jax import lax
from jax.experimental import pallas as pl
from jax.experimental.pallas import tpu as pltpu
from jax.sharding import Mesh, PartitionSpec as P

NROW = 16384
NCOL = 16384
RANK = 64
HIGH = lax.Precision.HIGHEST
COL = ("x", "y", "core")
NEAR = ("near",)
FAR = ("far",)
SIDE = 512
F32 = jnp.float32


def dot(a, b, dims):
    return lax.dot_general(
        a, b, (dims, ((), ())), precision=HIGH, preferred_element_type=F32
    )


def nn(a, b):
    return dot(a, b, ((1,), (0,)))


def nt(a, b):
    return dot(a, b, ((1,), (1,)))


def tn(a, b):
    return dot(a, b, ((0,), (0,)))


ANY = pl.BlockSpec(memory_space=pl.ANY)
VMEM = pl.BlockSpec(memory_space=pltpu.VMEM)


def call(kernel, outs, *args, far_in=(), far_out=(), scratch=()):
    args = [
        a if i in far_in else pltpu.with_memory_space_constraint(a, pltpu.VMEM)
        for i, a in enumerate(args)
    ]
    return pl.pallas_call(
        kernel,
        out_shape=[
            jax.ShapeDtypeStruct(s, d) if i in far_out else pltpu.VMEM(s, d)
            for i, (s, d) in enumerate(outs)
        ],
        in_specs=[ANY if i in far_in else VMEM for i in range(len(args))],
        out_specs=[ANY if i in far_out else VMEM for i in range(len(outs))],
        scratch_shapes=list(scratch),
        name=kernel.__name__,
    )(*args)


def write_tiles(ref, a):
    for i in range(8):
        for j in range(4):
            ref[4 * i + j] = a[8 * i : 8 * i + 8, 128 * j : 128 * j + 128]


def read_tiles(ref):
    rows = [jnp.concatenate([ref[4 * i + j] for j in range(4)], axis=1) for i in range(8)]
    return jnp.concatenate(rows, axis=0)


def places(shape):
    return lax.broadcasted_iota(jnp.int32, shape, 0), lax.broadcasted_iota(jnp.int32, shape, 1)


def fold(a):
    return jnp.concatenate([a[:32], a[32:]], axis=1)


def unfold(a):
    return jnp.concatenate([a[:, :64], a[:, 64:]], axis=0)


def factor(gram, width=8):
    row, lane = places((RANK, RANK))
    eye = jnp.where(row == lane, 1.0, 0.0).astype(F32)
    both = jnp.concatenate([gram, eye], axis=1)
    blocks = [both[8 * b : 8 * b + 8] for b in range(8)]
    in_block, _ = places((8, 128))
    for k in range(0, RANK, width):
        at, r = divmod(k, 8)
        columns = [
            {b: jnp.broadcast_to(blocks[b][:, k + j : k + j + 1], (8, 128)) for b in range(at, 8)}
            for j in range(width)
        ]
        lines = [blocks[at][r + j : r + j + 1] for j in range(width)]
        scaled = []
        for j in range(width):
            over = 1.0 / columns[j][at][r + j : r + j + 1]
            scaled.append(lines[j] * over)
            for l in range(j + 1, width):
                share = columns[j][at][r + l : r + l + 1] * over
                lines[l] = lines[l] - share * lines[j]
                for b in range(at, 8):
                    columns[l][b] = columns[l][b] - columns[j][b] * share
        for b in range(at, 8):
            new = blocks[b]
            for j in range(width):
                new = new - columns[j][b] * scaled[j]
            if b == at:
                new = jnp.where(in_block >= r + width, new, blocks[b])
                for j in range(width):
                    new = jnp.where(in_block == r + j, lines[j], new)
            blocks[b] = new
    both = jnp.concatenate(blocks, axis=0)
    upper, inverse = both[:, :64], both[:, 64:]
    pivot = jnp.sum(jnp.where(row == lane, upper, 0.0), axis=1, keepdims=True)
    root = 1.0 / jnp.sqrt(pivot)
    upper = jnp.where(row <= lane, upper * root, 0.0)
    return upper, inverse * root


STEPS = 4
STEP = SIDE // STEPS


def rows_of(i):
    return pl.ds(STEP * i, STEP)


def left_part(momentum, gradient, factor_t, part, blended, old, change, sems):
    copies = [
        pltpu.make_async_copy(momentum, old, sems.at[0]),
        pltpu.make_async_copy(gradient, change, sems.at[1]),
    ]
    for copy in copies:
        copy.start()
    for copy in copies:
        copy.wait()
    block = old[...] + change[...].astype(F32)
    blended[...] = block
    write_tiles(part, nt(factor_t[...], block))


def left_tile(parts, copies):
    tile = jnp.sum(parts[...], axis=0)
    for i in range(32):
        copies[i] = tile


def slices(a, axis, lead):
    bound = jnp.max(jnp.abs(a), axis=axis, keepdims=True)
    shift = bound * 2.0**lead
    parts = []
    for _ in range(4):
        part = (a + shift) - shift
        parts.append(part.astype(jnp.bfloat16))
        a = a - part
        shift = shift * 2.0 ** (lead - 25)
    return parts


def two_sum(a, b):
    total = a + b
    back = total - a
    return total, (a - (total - back)) + (b - back)


def total_of(terms):
    high, low = None, None
    for term in terms:
        a, b = term if isinstance(term, tuple) else (term, None)
        if high is None:
            high, low = a, (jnp.zeros_like(a) if b is None else b)
            continue
        high, error = two_sum(high, a)
        low = low + (error if b is None else error + b)
    top = high + low
    return top, low - (top - high)


def block_sum(blocks):
    wide = [
        total_of([blocks[64 * i : 64 * i + 64, 128 * j : 128 * j + 128] for i in range(4)])
        for j in range(2)
    ]
    high, low = total_of(wide)
    return total_of([(high[:, :64], low[:, :64]), (high[:, 64:], low[:, 64:])])


def exact(a, b, dims):
    return block_sum(
        lax.dot_general(a, b, (dims, ((), ())), preferred_element_type=F32)
    )


def right_part(tiles, blended, send):
    left_raw = read_tiles(tiles)
    product = nn(left_raw, blended[...])
    parts = jnp.concatenate(slices(left_raw, 1, 18), axis=0)
    high, low = exact(parts, parts, ((1,), (1,)))
    gram = jnp.concatenate([fold(high), fold(low)], axis=0)
    for i in range(8):
        for j in range(4):
            tile = product[8 * i : 8 * i + 8, 128 * j : 128 * j + 128]
            send[i // 2, 32 * (i % 2) + 8 * j : 32 * (i % 2) + 8 * j + 8] = tile
    for i in range(4):
        send[i, 64:] = gram


def sum_of(chunks, n, total):
    high, low = total_of([(chunks[i, 64:96], chunks[i, 96:128]) for i in range(n)])
    value = chunks[0, :64]
    for i in range(1, n):
        value = value + chunks[i, :64]
    total[:64] = value
    total[64:96] = high
    total[96:128] = low


def near_sum(chunks, total):
    sum_of(chunks, 4, total)


def far_sum(chunks, copies, gram):
    high, low = total_of([(chunks[i, 64:96], chunks[i, 96:128]) for i in range(8)])
    gram[:32] = high
    gram[32:] = low
    value = chunks[0, :64]
    for i in range(1, 8):
        value = value + chunks[i, :64]
    for i in range(4):
        copies[i] = value


def factors(gram, upper_one, inverse_one, inverse_two):
    high, low = unfold(gram[:32]), unfold(gram[32:])
    upper, inverse = factor(high)
    upper_one[...] = upper
    inverse_one[...] = inverse
    columns = jnp.concatenate(slices(upper, 0, 17), axis=1)
    square_high, square_low = exact(columns, columns, ((0,), (0,)))
    rest, error = two_sum(high, -square_high)
    rest = rest + (error + (low - square_low))
    lines = jnp.concatenate(slices(upper, 1, 17), axis=0)
    unit, _ = exact(jnp.concatenate(slices(inverse, 1, 17), axis=0), lines, ((1,), (1,)))
    gram_two = nt(unit, unit) + nt(nn(inverse, rest), inverse)
    _, second = factor(gram_two)
    inverse_two[...] = second


def right_of(total, inverse_one, inverse_two, right, copies):
    right_t = nn(inverse_two[...], nn(inverse_one[...], read_tiles(total)))
    right[...] = right_t
    squares = nt(jnp.ones((8, SIDE), F32), right_t * right_t)
    squares = jnp.concatenate([squares, jnp.zeros((8, 64), F32)], axis=1)
    for i in range(32):
        copies[i] = squares


def halves(a):
    high = a.astype(jnp.bfloat16)
    return high, (a - high.astype(F32)).astype(jnp.bfloat16)


def products(left_t, other, i):
    high, low = halves(left_t[:, STEP * i : STEP * i + STEP])
    lefts = jnp.concatenate([high, high, low], axis=0)
    high, low = halves(other)
    others = jnp.concatenate([high, low, high], axis=0)
    return lax.dot_general(
        lefts, others, (((0,), (0,)), ((), ())), preferred_element_type=F32
    )


def write_back(pairs, sems):
    copies = [pltpu.make_async_copy(a, b, sems.at[k]) for k, (a, b) in enumerate(pairs)]
    for copy in copies:
        copy.start()
    return copies


def momentum_of(tiles, inverse_one, inverse_two, right, blended, left, out, new_momentum, m, sems):
    left_t = nn(inverse_two[...], nn(inverse_one[...], read_tiles(tiles)))
    left[...] = left_t
    copies = write_back([(left, out)], sems.at[STEPS])
    scaled = 0.05 * right[...]
    for i in range(STEPS):
        m[rows_of(i)] = blended[rows_of(i)] - products(left_t, scaled, i)
        copies += write_back([(m.at[rows_of(i)], new_momentum.at[rows_of(i)])], sems.at[i])
    for copy in copies:
        copy.wait()


def update_of(parts, left, right, update, normed, u, n, sems):
    squares = parts[0, :1]
    for i in range(1, 32):
        squares = squares + parts[i, :1]
    row, lane = places((RANK, RANK))
    squares = jnp.sum(jnp.where(row == lane, squares[:, :64], 0.0), axis=1, keepdims=True)
    normed_t = right[...] / (jnp.sqrt(squares) + 1e-06)
    n[...] = normed_t
    copies = write_back([(n, normed)], sems.at[STEPS])
    scaled = math.sqrt(NROW * NCOL / RANK) * normed_t
    left_t = left[...]
    for i in range(STEPS):
        u[rows_of(i)] = products(left_t, scaled, i).astype(jnp.bfloat16)
        copies += write_back([(u.at[rows_of(i)], update.at[rows_of(i)])], sems.at[i])
    for copy in copies:
        copy.wait()


def exchange(chunks, axes):
    return lax.all_to_all(chunks, axes, 0, 0, tiled=True)


def on_device(momentum, gradient, right_factor):
    factor_t = right_factor.T
    flat, square, full = (RANK, SIDE), (RANK, RANK), (SIDE, SIDE)
    tiled = ((32, 8, 128), F32)
    part, blended = call(
        left_part,
        [tiled, (full, F32)],
        momentum, gradient, factor_t,
        far_in=(0, 1),
        scratch=[
            pltpu.VMEM(full, F32),
            pltpu.VMEM(full, jnp.bfloat16),
            pltpu.SemaphoreType.DMA((2,)),
        ],
    )
    (copies,) = call(left_tile, [tiled], exchange(part, COL))
    tiles = exchange(copies, COL)
    chunk = (128, 128)
    (send,) = call(right_part, [((4,) + chunk, F32)], tiles, blended)
    (near,) = call(near_sum, [(chunk, F32)], exchange(send, NEAR))
    quarters, gram = call(
        far_sum, [((4, 64, 128), F32), ((64, 128), F32)], lax.all_gather(near, FAR)
    )
    total = exchange(quarters, NEAR).reshape(32, 8, 128)
    upper_one, inverse_one, inverse_two = call(factors, [(square, F32)] * 3, gram)
    first_factor = upper_one.T / jnp.sqrt(F32(NROW) * F32(NCOL))
    right_t, copies = call(
        right_of, [(flat, F32), tiled], total, inverse_one, inverse_two
    )
    parts = exchange(copies, COL)
    left_in, left_t, new_momentum = call(
        momentum_of,
        [(flat, F32), (flat, F32), (full, F32)],
        tiles, inverse_one, inverse_two, right_t, blended,
        far_out=(1, 2),
        scratch=[pltpu.VMEM(full, F32), pltpu.SemaphoreType.DMA((STEPS + 1, 1))],
    )
    update, normed_t = call(
        update_of,
        [(full, jnp.bfloat16), (flat, F32)],
        parts, left_in, right_t,
        far_out=(0, 1),
        scratch=[
            pltpu.VMEM(full, jnp.bfloat16),
            pltpu.VMEM(flat, F32),
            pltpu.SemaphoreType.DMA((STEPS + 1, 1)),
        ],
    )
    return (update, left_t.T, normed_t.T, new_momentum, first_factor)


def solution(mesh):
    inner = Mesh(mesh.devices.reshape(8, 4, 4, 4, 2), FAR + NEAR + COL)
    row, col = FAR + NEAR, COL
    in_specs = (P(row, col), P(row, col), P(col, None))
    out_specs = (P(row, col), P(row, None), P(col, None), P(row, col), P())
    return jax.shard_map(
        on_device, mesh=inner, in_specs=in_specs, out_specs=out_specs, check_vma=False
    )
```

```python
import math

import jax
import jax.numpy as jnp
from jax import lax
from jax.experimental import pallas as pl
from jax.experimental.pallas import tpu as pltpu
from jax.sharding import Mesh, PartitionSpec as P

NROW = 16384
NCOL = 16384
RANK = 64
HIGH = lax.Precision.HIGHEST
COL = ("x", "y", "core")
NEAR = ("near",)
FAR = ("far",)
SIDE = 512
F32 = jnp.float32


def dot(a, b, dims):
    return lax.dot_general(
        a, b, (dims, ((), ())), precision=HIGH, preferred_element_type=F32
    )


def nn(a, b):
    return dot(a, b, ((1,), (0,)))


def nt(a, b):
    return dot(a, b, ((1,), (1,)))


def tn(a, b):
    return dot(a, b, ((0,), (0,)))


ANY = pl.BlockSpec(memory_space=pl.ANY)
VMEM = pl.BlockSpec(memory_space=pltpu.VMEM)


def call(kernel, outs, *args, far_in=(), far_out=(), scratch=()):
    args = [
        a if i in far_in else pltpu.with_memory_space_constraint(a, pltpu.VMEM)
        for i, a in enumerate(args)
    ]
    return pl.pallas_call(
        kernel,
        out_shape=[
            jax.ShapeDtypeStruct(s, d) if i in far_out else pltpu.VMEM(s, d)
            for i, (s, d) in enumerate(outs)
        ],
        in_specs=[ANY if i in far_in else VMEM for i in range(len(args))],
        out_specs=[ANY if i in far_out else VMEM for i in range(len(outs))],
        scratch_shapes=list(scratch),
        name=kernel.__name__,
    )(*args)


def write_tiles(ref, a):
    for i in range(8):
        for j in range(4):
            ref[4 * i + j] = a[8 * i : 8 * i + 8, 128 * j : 128 * j + 128]


def read_tiles(ref):
    rows = [jnp.concatenate([ref[4 * i + j] for j in range(4)], axis=1) for i in range(8)]
    return jnp.concatenate(rows, axis=0)


def places(shape):
    return lax.broadcasted_iota(jnp.int32, shape, 0), lax.broadcasted_iota(jnp.int32, shape, 1)


def fold(a):
    return jnp.concatenate([a[:32], a[32:]], axis=1)


def unfold(a):
    return jnp.concatenate([a[:, :64], a[:, 64:]], axis=0)


def factor(gram, width=8):
    row, lane = places((RANK, RANK))
    eye = jnp.where(row == lane, 1.0, 0.0).astype(F32)
    both = jnp.concatenate([gram, eye], axis=1)
    blocks = [both[8 * b : 8 * b + 8] for b in range(8)]
    in_block, _ = places((8, 128))
    for k in range(0, RANK, width):
        at, r = divmod(k, 8)
        columns = [
            {b: jnp.broadcast_to(blocks[b][:, k + j : k + j + 1], (8, 128)) for b in range(at, 8)}
            for j in range(width)
        ]
        lines = [blocks[at][r + j : r + j + 1] for j in range(width)]
        scaled = []
        for j in range(width):
            over = 1.0 / columns[j][at][r + j : r + j + 1]
            scaled.append(lines[j] * over)
            for l in range(j + 1, width):
                share = columns[j][at][r + l : r + l + 1] * over
                lines[l] = lines[l] - share * lines[j]
                for b in range(at, 8):
                    columns[l][b] = columns[l][b] - columns[j][b] * share
        for b in range(at, 8):
            new = blocks[b]
            for j in range(width):
                new = new - columns[j][b] * scaled[j]
            if b == at:
                new = jnp.where(in_block >= r + width, new, blocks[b])
                for j in range(width):
                    new = jnp.where(in_block == r + j, lines[j], new)
            blocks[b] = new
    both = jnp.concatenate(blocks, axis=0)
    upper, inverse = both[:, :64], both[:, 64:]
    pivot = jnp.sum(jnp.where(row == lane, upper, 0.0), axis=1, keepdims=True)
    root = 1.0 / jnp.sqrt(pivot)
    upper = jnp.where(row <= lane, upper * root, 0.0)
    return upper, inverse * root


STEPS = 4
STEP = SIDE // STEPS


def rows_of(i):
    return pl.ds(STEP * i, STEP)


def start_copies(pairs, sems):
    copies = [pltpu.make_async_copy(a, b, sems.at[k]) for k, (a, b) in enumerate(pairs)]
    for copy in copies:
        copy.start()
    return copies


def left_part(momentum, gradient, factor_t, part, blended, old, change, right, sems):
    pairs = ((momentum, old), (gradient, change), (factor_t, right))
    for copy in start_copies(pairs, sems):
        copy.wait()
    block = old[...] + change[...].astype(F32)
    blended[...] = block
    write_tiles(part, nt(right[...], block))


def left_tile(parts, copies):
    tile = jnp.sum(parts[...], axis=0)
    for i in range(32):
        copies[i] = tile


def slices(a, axis, lead):
    bound = jnp.max(jnp.abs(a), axis=axis, keepdims=True)
    shift = bound * 2.0**lead
    parts = []
    for _ in range(4):
        part = (a + shift) - shift
        parts.append(part.astype(jnp.bfloat16))
        a = a - part
        shift = shift * 2.0 ** (lead - 25)
    return parts


def two_sum(a, b):
    total = a + b
    back = total - a
    return total, (a - (total - back)) + (b - back)


def total_of(terms):
    high, low = None, None
    for term in terms:
        a, b = term if isinstance(term, tuple) else (term, None)
        if high is None:
            high, low = a, (jnp.zeros_like(a) if b is None else b)
            continue
        high, error = two_sum(high, a)
        low = low + (error if b is None else error + b)
    top = high + low
    return top, low - (top - high)


def block_sum(blocks):
    wide = [
        total_of([blocks[64 * i : 64 * i + 64, 128 * j : 128 * j + 128] for i in range(4)])
        for j in range(2)
    ]
    high, low = total_of(wide)
    return total_of([(high[:, :64], low[:, :64]), (high[:, 64:], low[:, 64:])])


def exact(a, b, dims):
    return block_sum(
        lax.dot_general(a, b, (dims, ((), ())), preferred_element_type=F32)
    )


def right_part(tiles, blended, send):
    left_raw = read_tiles(tiles)
    product = nn(left_raw, blended[...])
    parts = jnp.concatenate(slices(left_raw, 1, 18), axis=0)
    high, low = exact(parts, parts, ((1,), (1,)))
    gram = jnp.concatenate([fold(high), fold(low)], axis=0)
    for i in range(8):
        for j in range(4):
            tile = product[8 * i : 8 * i + 8, 128 * j : 128 * j + 128]
            send[i // 2, 32 * (i % 2) + 8 * j : 32 * (i % 2) + 8 * j + 8] = tile
    for i in range(4):
        send[i, 64:] = gram


def sum_of(chunks, n, total):
    high, low = total_of([(chunks[i, 64:96], chunks[i, 96:128]) for i in range(n)])
    value = chunks[0, :64]
    for i in range(1, n):
        value = value + chunks[i, :64]
    total[:64] = value
    total[64:96] = high
    total[96:128] = low


def near_sum(chunks, total):
    sum_of(chunks, 4, total)


def far_sum(chunks, copies, gram):
    high, low = total_of([(chunks[i, 64:96], chunks[i, 96:128]) for i in range(8)])
    gram[:32] = high
    gram[32:] = low
    value = chunks[0, :64]
    for i in range(1, 8):
        value = value + chunks[i, :64]
    for i in range(4):
        copies[i] = value


def factors(gram, upper_one, inverse_one, inverse_two):
    high, low = unfold(gram[:32]), unfold(gram[32:])
    upper, inverse = factor(high)
    upper_one[...] = upper
    inverse_one[...] = inverse
    columns = jnp.concatenate(slices(upper, 0, 17), axis=1)
    square_high, square_low = exact(columns, columns, ((0,), (0,)))
    rest, error = two_sum(high, -square_high)
    rest = rest + (error + (low - square_low))
    lines = jnp.concatenate(slices(upper, 1, 17), axis=0)
    unit, _ = exact(jnp.concatenate(slices(inverse, 1, 17), axis=0), lines, ((1,), (1,)))
    gram_two = nt(unit, unit) + nt(nn(inverse, rest), inverse)
    _, second = factor(gram_two)
    inverse_two[...] = second


def right_of(total, inverse_one, inverse_two, right, copies):
    right_t = nn(inverse_two[...], nn(inverse_one[...], read_tiles(total)))
    right[...] = right_t
    squares = nt(jnp.ones((8, SIDE), F32), right_t * right_t)
    squares = jnp.concatenate([squares, jnp.zeros((8, 64), F32)], axis=1)
    for i in range(4):
        copies[8 * i : 8 * i + 8] = squares


def halves(a):
    high = a.astype(jnp.bfloat16)
    return high, (a - high.astype(F32)).astype(jnp.bfloat16)


def products(left_t, other, i):
    high, low = halves(left_t[:, STEP * i : STEP * i + STEP])
    lefts = jnp.concatenate([high, high, low], axis=0)
    high, low = halves(other)
    others = jnp.concatenate([high, low, high], axis=0)
    return lax.dot_general(
        lefts, others, (((0,), (0,)), ((), ())), preferred_element_type=F32
    )


def momentum_of(tiles, inverse_one, inverse_two, right, blended, left, out, new_momentum, m, sems):
    left_t = nn(inverse_two[...], nn(inverse_one[...], read_tiles(tiles)))
    left[...] = left_t
    copies = start_copies([(left, out)], sems.at[STEPS])
    scaled = 0.05 * right[...]
    for i in range(STEPS):
        m[rows_of(i)] = blended[rows_of(i)] - products(left_t, scaled, i)
        copies += start_copies([(m.at[rows_of(i)], new_momentum.at[rows_of(i)])], sems.at[i])
    for copy in copies:
        copy.wait()


def update_of(parts, left, right, update, normed, u, n, sems):
    squares = jnp.sum(parts[...], axis=0, keepdims=True)
    row, lane = places((RANK, RANK))
    squares = jnp.sum(jnp.where(row == lane, squares[:, :64], 0.0), axis=1, keepdims=True)
    normed_t = right[...] / (jnp.sqrt(squares) + 1e-06)
    n[...] = normed_t
    copies = start_copies([(n, normed)], sems.at[STEPS])
    scaled = math.sqrt(NROW * NCOL / RANK) * normed_t
    left_t = left[...]
    for i in range(STEPS):
        u[rows_of(i)] = products(left_t, scaled, i).astype(jnp.bfloat16)
        copies += start_copies([(u.at[rows_of(i)], update.at[rows_of(i)])], sems.at[i])
    for copy in copies:
        copy.wait()


def exchange(chunks, axes):
    return lax.all_to_all(chunks, axes, 0, 0, tiled=True)


def on_device(momentum, gradient, right_factor):
    factor_t = right_factor.T
    flat, square, full = (RANK, SIDE), (RANK, RANK), (SIDE, SIDE)
    tiled = ((32, 8, 128), F32)
    part, blended = call(
        left_part,
        [tiled, (full, F32)],
        momentum, gradient, factor_t,
        far_in=(0, 1, 2),
        scratch=[
            pltpu.VMEM(full, F32),
            pltpu.VMEM(full, jnp.bfloat16),
            pltpu.VMEM(flat, F32),
            pltpu.SemaphoreType.DMA((3,)),
        ],
    )
    (copies,) = call(left_tile, [tiled], exchange(part, COL))
    tiles = exchange(copies, COL)
    chunk = (128, 128)
    (send,) = call(right_part, [((4,) + chunk, F32)], tiles, blended)
    (near,) = call(near_sum, [(chunk, F32)], exchange(send, NEAR))
    quarters, gram = call(
        far_sum, [((4, 64, 128), F32), ((64, 128), F32)], lax.all_gather(near, FAR)
    )
    total = exchange(quarters, NEAR).reshape(32, 8, 128)
    upper_one, inverse_one, inverse_two = call(factors, [(square, F32)] * 3, gram)
    first_factor = upper_one.T / jnp.sqrt(F32(NROW) * F32(NCOL))
    right_t, copies = call(
        right_of, [(flat, F32), ((32, 128), F32)], total, inverse_one, inverse_two
    )
    parts = exchange(copies.reshape(32, 1, 128), COL).reshape(32, 128)
    left_in, left_t, new_momentum = call(
        momentum_of,
        [(flat, F32), (flat, F32), (full, F32)],
        tiles, inverse_one, inverse_two, right_t, blended,
        far_out=(1, 2),
        scratch=[pltpu.VMEM(full, F32), pltpu.SemaphoreType.DMA((STEPS + 1, 1))],
    )
    update, normed_t = call(
        update_of,
        [(full, jnp.bfloat16), (flat, F32)],
        parts, left_in, right_t,
        far_out=(0, 1),
        scratch=[
            pltpu.VMEM(full, jnp.bfloat16),
            pltpu.VMEM(flat, F32),
            pltpu.SemaphoreType.DMA((STEPS + 1, 1)),
        ],
    )
    return (update, left_t.T, normed_t.T, new_momentum, first_factor)


def solution(mesh):
    inner = Mesh(mesh.devices.reshape(8, 4, 4, 4, 2), FAR + NEAR + COL)
    row, col = FAR + NEAR, COL
    in_specs = (P(row, col), P(row, col), P(col, None))
    out_specs = (P(row, col), P(row, None), P(col, None), P(row, col), P())
    return jax.shard_map(
        on_device, mesh=inner, in_specs=in_specs, out_specs=out_specs, check_vma=False
    )
```

```python
import math

import jax
import jax.numpy as jnp
from jax import lax
from jax.experimental import pallas as pl
from jax.experimental.pallas import tpu as pltpu
from jax.sharding import Mesh, PartitionSpec as P

NROW = 16384
NCOL = 16384
RANK = 64
HIGH = lax.Precision.HIGHEST
COL = ("x", "y", "core")
NEAR = ("near",)
FAR = ("far",)
SIDE = 512
F32 = jnp.float32


def dot(a, b, dims):
    return lax.dot_general(
        a, b, (dims, ((), ())), precision=HIGH, preferred_element_type=F32
    )


def nn(a, b):
    return dot(a, b, ((1,), (0,)))


def nt(a, b):
    return dot(a, b, ((1,), (1,)))


def tn(a, b):
    return dot(a, b, ((0,), (0,)))


ANY = pl.BlockSpec(memory_space=pl.ANY)
VMEM = pl.BlockSpec(memory_space=pltpu.VMEM)


def call(kernel, outs, *args, far_in=(), far_out=(), scratch=()):
    args = [
        a if i in far_in else pltpu.with_memory_space_constraint(a, pltpu.VMEM)
        for i, a in enumerate(args)
    ]
    return pl.pallas_call(
        kernel,
        out_shape=[
            jax.ShapeDtypeStruct(s, d) if i in far_out else pltpu.VMEM(s, d)
            for i, (s, d) in enumerate(outs)
        ],
        in_specs=[ANY if i in far_in else VMEM for i in range(len(args))],
        out_specs=[ANY if i in far_out else VMEM for i in range(len(outs))],
        scratch_shapes=list(scratch),
        name=kernel.__name__,
    )(*args)


def write_tiles(ref, a):
    for i in range(8):
        for j in range(4):
            ref[4 * i + j] = a[8 * i : 8 * i + 8, 128 * j : 128 * j + 128]


def read_tiles(ref):
    rows = [jnp.concatenate([ref[4 * i + j] for j in range(4)], axis=1) for i in range(8)]
    return jnp.concatenate(rows, axis=0)


def places(shape):
    return lax.broadcasted_iota(jnp.int32, shape, 0), lax.broadcasted_iota(jnp.int32, shape, 1)


def fold(a):
    return jnp.concatenate([a[:32], a[32:]], axis=1)


def unfold(a):
    return jnp.concatenate([a[:, :64], a[:, 64:]], axis=0)


def factor(gram, width=8):
    row, lane = places((RANK, RANK))
    eye = jnp.where(row == lane, 1.0, 0.0).astype(F32)
    both = jnp.concatenate([gram, eye], axis=1)
    blocks = [both[8 * b : 8 * b + 8] for b in range(8)]
    in_block, _ = places((8, 128))
    for k in range(0, RANK, width):
        at, r = divmod(k, 8)
        columns = [
            {b: jnp.broadcast_to(blocks[b][:, k + j : k + j + 1], (8, 128)) for b in range(at, 8)}
            for j in range(width)
        ]
        lines = [blocks[at][r + j : r + j + 1] for j in range(width)]
        scaled = []
        for j in range(width):
            over = 1.0 / columns[j][at][r + j : r + j + 1]
            scaled.append(lines[j] * over)
            for l in range(j + 1, width):
                share = columns[j][at][r + l : r + l + 1] * over
                lines[l] = lines[l] - share * lines[j]
                for b in range(at, 8):
                    columns[l][b] = columns[l][b] - columns[j][b] * share
        for b in range(at, 8):
            new = blocks[b]
            for j in range(width):
                new = new - columns[j][b] * scaled[j]
            if b == at:
                new = jnp.where(in_block >= r + width, new, blocks[b])
                for j in range(width):
                    new = jnp.where(in_block == r + j, lines[j], new)
            blocks[b] = new
    both = jnp.concatenate(blocks, axis=0)
    upper, inverse = both[:, :64], both[:, 64:]
    pivot = jnp.sum(jnp.where(row == lane, upper, 0.0), axis=1, keepdims=True)
    root = 1.0 / jnp.sqrt(pivot)
    upper = jnp.where(row <= lane, upper * root, 0.0)
    return upper, inverse * root


STEPS = 4
STEP = SIDE // STEPS


def rows_of(i):
    return pl.ds(STEP * i, STEP)


def start_copies(pairs, sems):
    copies = [pltpu.make_async_copy(a, b, sems.at[k]) for k, (a, b) in enumerate(pairs)]
    for copy in copies:
        copy.start()
    return copies


def left_part(momentum, gradient, factor_t, part, blended, old, change, right, sems):
    pairs = ((momentum, old), (gradient, change), (factor_t, right))
    for copy in start_copies(pairs, sems):
        copy.wait()
    block = old[...] + change[...].astype(F32)
    blended[...] = block
    write_tiles(part, nt(right[...], block))


def left_tile(parts, copies):
    tile = jnp.sum(parts[...], axis=0)
    for i in range(32):
        copies[i] = tile


def slices(a, axis, lead):
    bound = jnp.max(jnp.abs(a), axis=axis, keepdims=True)
    shift = bound * 2.0**lead
    parts = []
    for _ in range(4):
        part = (a + shift) - shift
        parts.append(part.astype(jnp.bfloat16))
        a = a - part
        shift = shift * 2.0 ** (lead - 25)
    return parts


def two_sum(a, b):
    total = a + b
    back = total - a
    return total, (a - (total - back)) + (b - back)


def total_of(terms):
    high, low = None, None
    for term in terms:
        a, b = term if isinstance(term, tuple) else (term, None)
        if high is None:
            high, low = a, (jnp.zeros_like(a) if b is None else b)
            continue
        high, error = two_sum(high, a)
        low = low + (error if b is None else error + b)
    top = high + low
    return top, low - (top - high)


def block_sum(blocks):
    wide = [
        total_of([blocks[64 * i : 64 * i + 64, 128 * j : 128 * j + 128] for i in range(4)])
        for j in range(2)
    ]
    high, low = total_of(wide)
    return total_of([(high[:, :64], low[:, :64]), (high[:, 64:], low[:, 64:])])


def exact(a, b, dims):
    return block_sum(
        lax.dot_general(a, b, (dims, ((), ())), preferred_element_type=F32)
    )


def right_part(tiles, blended, send):
    left_raw = read_tiles(tiles)
    product = nn(left_raw, blended[...])
    parts = jnp.concatenate(slices(left_raw, 1, 18), axis=0)
    high, low = exact(parts, parts, ((1,), (1,)))
    gram = jnp.concatenate([fold(high), fold(low)], axis=0)
    for i in range(8):
        for j in range(4):
            tile = product[8 * i : 8 * i + 8, 128 * j : 128 * j + 128]
            send[i // 2, 32 * (i % 2) + 8 * j : 32 * (i % 2) + 8 * j + 8] = tile
    for i in range(4):
        send[i, 64:] = gram


def value_sum(chunks, n):
    value = chunks[0, :64]
    for i in range(1, n):
        value = value + chunks[i, :64]
    return value


def near_sum(chunks, total):
    high, low = total_of([(chunks[i, 64:96], chunks[i, 96:128]) for i in range(4)])
    high, low = unfold(high), unfold(low)
    row, lane = places((RANK, RANK))
    diagonal = jnp.sum(jnp.where(row == lane, low, 0.0), axis=0, keepdims=True)
    diagonal = jnp.concatenate([diagonal, jnp.zeros((1, 64), F32)], axis=1)
    total[:64] = value_sum(chunks, 4)
    total[64:96] = fold(jnp.where(row <= lane, high, low.T))
    total[96:] = jnp.broadcast_to(diagonal, (8, 128))


def far_sum(chunks, copies, gram):
    value = value_sum(chunks, 8)
    for i in range(4):
        copies[i] = value
    high, error = total_of([chunks[i, 64:96] for i in range(8)])
    gram[:32] = high
    gram[32:64] = error
    diagonal = chunks[0, 96:]
    for i in range(1, 8):
        diagonal = diagonal + chunks[i, 96:]
    gram[64:] = diagonal


def factors(gram, upper_one, inverse_one, inverse_two):
    packed, error = unfold(gram[:32]), unfold(gram[32:64])
    row, lane = places((RANK, RANK))
    flipped = packed.T
    high = jnp.where(row <= lane, packed, flipped)
    low = error + jnp.where(row == lane, gram[64:65, :64], flipped)
    low = jnp.where(row <= lane, low, low.T)
    upper, inverse = factor(high)
    upper_one[...] = upper
    inverse_one[...] = inverse
    columns = jnp.concatenate(slices(upper, 0, 17), axis=1)
    square_high, square_low = exact(columns, columns, ((0,), (0,)))
    rest, error = two_sum(high, -square_high)
    rest = rest + (error + (low - square_low))
    lines = jnp.concatenate(slices(upper, 1, 17), axis=0)
    unit, _ = exact(jnp.concatenate(slices(inverse, 1, 17), axis=0), lines, ((1,), (1,)))
    gram_two = nt(unit, unit) + nt(nn(inverse, rest), inverse)
    _, second = factor(gram_two)
    inverse_two[...] = second


def right_of(total, inverse_one, inverse_two, right, copies):
    right_t = nn(inverse_two[...], nn(inverse_one[...], read_tiles(total)))
    right[...] = right_t
    squares = nt(jnp.ones((8, SIDE), F32), right_t * right_t)
    squares = jnp.concatenate([squares, jnp.zeros((8, 64), F32)], axis=1)
    for i in range(4):
        copies[8 * i : 8 * i + 8] = squares


def halves(a):
    high = a.astype(jnp.bfloat16)
    return high, (a - high.astype(F32)).astype(jnp.bfloat16)


def products(left_t, other, i):
    high, low = halves(left_t[:, STEP * i : STEP * i + STEP])
    lefts = jnp.concatenate([high, high, low], axis=0)
    high, low = halves(other)
    others = jnp.concatenate([high, low, high], axis=0)
    return lax.dot_general(
        lefts, others, (((0,), (0,)), ((), ())), preferred_element_type=F32
    )


def momentum_of(tiles, inverse_one, inverse_two, right, blended, left, out, new_momentum, m, sems):
    left_t = nn(inverse_two[...], nn(inverse_one[...], read_tiles(tiles)))
    left[...] = left_t
    copies = start_copies([(left, out)], sems.at[STEPS])
    scaled = 0.05 * right[...]
    for i in range(STEPS):
        m[rows_of(i)] = blended[rows_of(i)] - products(left_t, scaled, i)
        copies += start_copies([(m.at[rows_of(i)], new_momentum.at[rows_of(i)])], sems.at[i])
    for copy in copies:
        copy.wait()


def update_of(parts, left, right, update, normed, u, n, sems):
    squares = jnp.sum(parts[...], axis=0, keepdims=True)
    row, lane = places((RANK, RANK))
    squares = jnp.sum(jnp.where(row == lane, squares[:, :64], 0.0), axis=1, keepdims=True)
    normed_t = right[...] / (jnp.sqrt(squares) + 1e-06)
    n[...] = normed_t
    copies = start_copies([(n, normed)], sems.at[STEPS])
    scaled = math.sqrt(NROW * NCOL / RANK) * normed_t
    left_t = left[...]
    for i in range(STEPS):
        u[rows_of(i)] = products(left_t, scaled, i).astype(jnp.bfloat16)
        copies += start_copies([(u.at[rows_of(i)], update.at[rows_of(i)])], sems.at[i])
    for copy in copies:
        copy.wait()


def exchange(chunks, axes):
    return lax.all_to_all(chunks, axes, 0, 0, tiled=True)


def on_device(momentum, gradient, right_factor):
    factor_t = right_factor.T
    flat, square, full = (RANK, SIDE), (RANK, RANK), (SIDE, SIDE)
    tiled = ((32, 8, 128), F32)
    part, blended = call(
        left_part,
        [tiled, (full, F32)],
        momentum, gradient, factor_t,
        far_in=(0, 1, 2),
        scratch=[
            pltpu.VMEM(full, F32),
            pltpu.VMEM(full, jnp.bfloat16),
            pltpu.VMEM(flat, F32),
            pltpu.SemaphoreType.DMA((3,)),
        ],
    )
    (copies,) = call(left_tile, [tiled], exchange(part, COL))
    tiles = exchange(copies, COL)
    (send,) = call(right_part, [((4, 128, 128), F32)], tiles, blended)
    (near,) = call(near_sum, [((104, 128), F32)], exchange(send, NEAR))
    quarters, gram = call(
        far_sum, [((4, 64, 128), F32), ((72, 128), F32)], lax.all_gather(near, FAR)
    )
    total = exchange(quarters, NEAR).reshape(32, 8, 128)
    upper_one, inverse_one, inverse_two = call(factors, [(square, F32)] * 3, gram)
    first_factor = upper_one.T / jnp.sqrt(F32(NROW) * F32(NCOL))
    right_t, copies = call(
        right_of, [(flat, F32), ((32, 128), F32)], total, inverse_one, inverse_two
    )
    parts = exchange(copies.reshape(32, 1, 128), COL).reshape(32, 128)
    left_in, left_t, new_momentum = call(
        momentum_of,
        [(flat, F32), (flat, F32), (full, F32)],
        tiles, inverse_one, inverse_two, right_t, blended,
        far_out=(1, 2),
        scratch=[pltpu.VMEM(full, F32), pltpu.SemaphoreType.DMA((STEPS + 1, 1))],
    )
    update, normed_t = call(
        update_of,
        [(full, jnp.bfloat16), (flat, F32)],
        parts, left_in, right_t,
        far_out=(0, 1),
        scratch=[
            pltpu.VMEM(full, jnp.bfloat16),
            pltpu.VMEM(flat, F32),
            pltpu.SemaphoreType.DMA((STEPS + 1, 1)),
        ],
    )
    return (update, left_t.T, normed_t.T, new_momentum, first_factor)


def solution(mesh):
    inner = Mesh(mesh.devices.reshape(8, 4, 4, 4, 2), FAR + NEAR + COL)
    row, col = FAR + NEAR, COL
    in_specs = (P(row, col), P(row, col), P(col, None))
    out_specs = (P(row, col), P(row, None), P(col, None), P(row, col), P())
    return jax.shard_map(
        on_device, mesh=inner, in_specs=in_specs, out_specs=out_specs, check_vma=False
    )
```
